512 devices in a mesh: ctx: 32 (over z, y_lo), exp: 16 (over y_hi, x, core).
Axes of the slice: x: 4, y: 4 (y_hi: 2, y_lo: 2; y = y_hi * 2 + y_lo), z: 16, core: 2. Of those that a mesh axis runs over, the one named last changes fastest.
Arguments:
- queries: bfloat16 [4096, 64, 576], P('ctx', 'exp'), may hold values from -300 to 300
- latents: bfloat16 [4096, 576], P('ctx'), may hold values from -6 to 6
- value_up: bfloat16 [64, 512, 128], P('exp'), may hold values from -0.5 to 0.5
- out_weight: bfloat16 [8192, 7168], P('exp', 'ctx'), may hold values from -0.125 to 0.125
Outputs:
- attn_out: bfloat16 [4096, 7168], P(('ctx', 'exp'))
The draws below stay inside these ranges and needn't reach their ends.
All inputs are finite; a program needn't handle non-finite values.
Results may differ from the reference program's by a relative error of at most 0.014.
Values may be sent and summed in bfloat16 or wider, within the bound.
A program may use at most 64 MiB of HBM per device.

```python
import jax
import jax.numpy as jnp
from jax import lax

D = 7168
LAT = 576
VLAT = 512
VD = 128
HEADS = 64
TOKENS = 4096


def shared_fields(key):
    base = jax.random.fold_in(key, 11)
    key_a, key_b = jax.random.split(base, 2)
    latent_rows = jnp.clip(jax.random.normal(key_a, (TOKENS, LAT), jnp.float32), -6.0, 6.0)
    query_rows = jnp.clip(jax.random.normal(key_b, (TOKENS, HEADS, LAT), jnp.float32), -6.0, 6.0)
    return (query_rows, latent_rows)


def draw_queries(key, part):
    query_rows, latent_rows = shared_fields(key)
    return query_rows.astype(jnp.bfloat16)


def draw_latents(key, part):
    query_rows, latent_rows = shared_fields(key)
    return latent_rows.astype(jnp.bfloat16)


def level_of(own_key, shape, cuts, smallest, high):
    def one(dim, shards_of):
        draws = jax.random.uniform(jax.random.fold_in(jax.random.fold_in(own_key, 6), dim), (shards_of,), jnp.float32, smallest / len(cuts), high / len(cuts))
        return jnp.repeat(jnp.exp(draws), shape[dim] // shards_of).reshape((-1,) + (1,) * (len(shape) - dim - 1))

    factor_of = one(*cuts[0])
    for cut in cuts[1:]:
        factor_of = factor_of * one(*cut)
    return factor_of


def scatter_about(key, dims, spread, limit, cuts=(), dtype=jnp.bfloat16):
    entries = spread * jax.random.normal(key, dims, jnp.float32)
    if cuts:
        entries = entries * level_of(key, dims, cuts, -0.22, 0.18)
    return jnp.clip(entries, -limit, limit).astype(dtype)


def setup_inputs(seed: int = 0) -> dict:
    key_of = jax.random.split(jax.random.key(seed), 5)
    return {
        "queries": draw_queries(jax.random.fold_in(key_of[4], 71), 0),
        "latents": draw_latents(jax.random.fold_in(key_of[4], 71), 0),
        "value_up": scatter_about(key_of[2], (HEADS, VLAT, VD), (VLAT // 4) ** -0.5, 0.5, ((0, 16),)),
        "out_weight": scatter_about(key_of[3], (HEADS * VD, D), (HEADS * VD // 4) ** -0.5, 0.125, ((0, 16), (1, 32))),
    }


score_scale = 192.0 ** -0.5


def reference(queries, latents, value_up, out_weight):
    position = jnp.arange(TOKENS)
    visible = position[None, :] <= position[:, None]
    value_part = latents[:, :VLAT]

    def one_head(pair):
        head_query, head_up = pair
        scores = jnp.dot(head_query, latents.T, preferred_element_type=jnp.float32) * score_scale
        scores = jnp.where(visible, scores, -jnp.inf)
        top = jnp.max(scores, axis=1, keepdims=True)
        expo = jnp.where(visible, jnp.exp(scores - top), 0.0)
        total = jnp.sum(expo, axis=1, keepdims=True)
        weights = expo.astype(jnp.bfloat16)
        context = (jnp.dot(weights, value_part, preferred_element_type=jnp.float32) / total).astype(jnp.bfloat16)
        return jnp.dot(context, head_up, preferred_element_type=jnp.float32).astype(jnp.bfloat16)

    per_head = lax.map(one_head, (jnp.moveaxis(queries, 1, 0), value_up))
    values = jnp.moveaxis(per_head, 0, 1).reshape(TOKENS, HEADS * VD)
    return jnp.dot(values, out_weight, preferred_element_type=jnp.float32).astype(jnp.bfloat16)
```

```python
import functools

import jax
import jax.numpy as jnp
from jax import lax
from jax.experimental import pallas as pl
from jax.experimental.pallas import tpu as pltpu
from jax.sharding import PartitionSpec as P

MESH = pl.DeviceIdType.MESH
LANES = 128
GROUP = 4
LOG2E = 1.4426950408889634
score_scale = 192.0 ** (-0.5)
LOW = -1e30


def kernel(
    nz, nx, nvl, nb,
    q_ref, lat_ref, up_ref, w_ref, out_ref,
    lat_s, wab, m_s, l_s, acc, vx, ps, cr, xs, xr, ys, yr,
    zl_s, zl_r, yf_s, yf_r, ce_s, ce_r, co_s, co_r,
    za_s, za_r, zb_s, zb_r, v_s, v_r, c_s, c_r, x_s, x_r, y_s, y_r,
):
    half = nz // 2
    tok = lat_ref.shape[0]
    hrow = tok // 2
    heads = up_ref.shape[0]
    vd = up_ref.shape[2]
    sub = nb // 2
    n_a = nz // GROUP
    n_groups = 2 * n_a

    ctx, ex = lax.axis_index("ctx"), lax.axis_index("exp")
    z, yl = ctx // 2, ctx % 2
    yh, x, k = ex // (2 * nx), (ex // 2) % nx, ex % 2
    y = yh * 2 + yl

    def dev(zz=z, yy=y, xx=x, kk=k):
        return {"ctx": zz * 2 + yy % 2, "exp": (yy // 2) * (2 * nx) + xx * 2 + kk}

    zn = (dev(zz=(z + 1) % nz), dev(zz=(z + nz - 1) % nz))
    yn = (dev(yy=(y + 1) % 4), dev(yy=(y + 3) % 4))
    core = dev(kk=1 - k)
    ypair = dev(yy=yh * 2 + 1 - yl)
    xn = tuple(((x + dx) % nx, dev(xx=(x + dx) % nx)) for dx in range(1, nx))
    y4 = tuple(((y + dy) % 4, dev(yy=(y + dy) % 4)) for dy in range(1, 4))

    def rc(src, dst, ss, rs, to):
        return pltpu.make_async_remote_copy(
            src_ref=src, dst_ref=dst, send_sem=ss, recv_sem=rs, device_id=to, device_id_type=MESH
        )

    def zc(d, s):
        return (z + nz - s) % nz if d == 0 else (z + s) % nz

    def slot(c, yy, kk):
        return lat_s.at[c, pl.ds(pl.multiple_of(yy * tok + kk * hrow, hrow), hrow)]

    own_half = lat_ref.at[pl.ds(pl.multiple_of(k * hrow, hrow), hrow)]

    def zl(d, s, src=None):
        at = slot(zc(d, s), yl, k)
        return rc(at if src is None else src, at, zl_s.at[d, s], zl_r.at[d, s], zn[d])

    def zl_in(d, s):
        at = slot(zc(d, s), yl, k)
        return rc(at, at, zl_s.at[d, s - 1], zl_r.at[d, s - 1], zn[d])

    def yf(d, s, src=None):
        at = slot(zc(d, s), yl, k)
        return rc(at if src is None else src, at, yf_s.at[d, s], yf_r.at[d, s], yn[d])

    def yf_in(d, s):
        at = slot(zc(d, s), 1 - yl, k)
        return rc(at, at, yf_s.at[d, s], yf_r.at[d, s], yn[d])

    def ce(d, s):
        at = slot(zc(d, s), yl, k)
        return rc(at, at, ce_s.at[d, s], ce_r.at[d, s], core)

    def ce_in(d, s):
        at = slot(zc(d, s), yl, 1 - k)
        return rc(at, at, ce_s.at[d, s], ce_r.at[d, s], core)

    def co(d, s):
        at = slot(zc(d, s), 1 - yl, k)
        return rc(at, at, co_s.at[d, s], co_r.at[d, s], core)

    def co_in(d, s):
        at = slot(zc(d, s), 1 - yl, 1 - k)
        return rc(at, at, co_s.at[d, s], co_r.at[d, s], core)

    def za(d, s, src=None, back=0):
        at = wab.at[0, zc(d, s)]
        return rc(at if src is None else src, at, za_s.at[d, s - back], za_r.at[d, s - back], zn[d])

    def zb(d, p, s, src=None, back=0):
        at = wab.at[1, zc(d, s), pl.ds(p * sub, sub)]
        return rc(
            at if src is None else src, at, zb_s.at[d, p, s - back], zb_r.at[d, p, s - back], zn[d]
        )

    barrier = pltpu.get_barrier_semaphore()
    peers = [zn[0], zn[1], core] + [t for _, t in xn] + [t for _, t in y4]
    for peer in peers:
        pl.semaphore_signal(barrier, inc=1, device_id=peer, device_id_type=MESH)
    pl.semaphore_wait(barrier, len(peers))

    for d in range(2):
        zl(d, 0, own_half).start()
    yf(0, 0, own_half).start()
    for d in range(2):
        za(d, 0, w_ref.at[0]).start()

    lat_s[z, pl.ds(pl.multiple_of(yl * tok, tok), tok)] = lat_ref[...]
    wab[0, z] = w_ref[0]
    wab[1, z] = w_ref[1]
    if nb < LANES:
        wab[1, :, nb:] = jnp.zeros((nz, LANES - nb, wab.shape[3]), wab.dtype)
    m_s[...] = jnp.full_like(m_s, LOW)
    l_s[...] = jnp.zeros_like(l_s)
    acc[...] = jnp.zeros_like(acc)

    def attend(c):
        keys = lat_s[c]
        scores = lax.dot_general(
            q_ref[...], keys, (((1,), (1,)), ((), ())), preferred_element_type=jnp.float32
        ) * (score_scale * LOG2E)
        rows, cols = scores.shape
        row_pos = z * cols + yl * tok + lax.broadcasted_iota(jnp.int32, (rows, cols), 0) % tok
        key_pos = c * cols + lax.broadcasted_iota(jnp.int32, (rows, cols), 1)
        scores = jnp.where(key_pos <= row_pos, scores, LOW)
        old = m_s[...]
        new = jnp.maximum(old, jnp.max(scores, axis=1, keepdims=True))
        shrink = jnp.exp2(old - new)
        expo = jnp.exp2(scores - new)
        m_s[...] = new
        l_s[...] = l_s[...] * shrink + jnp.sum(expo, axis=1, keepdims=True)
        acc[...] = acc[...] * shrink + jnp.dot(
            expo.astype(jnp.bfloat16), keys[:, :nvl], preferred_element_type=jnp.float32
        )

    def relay_b(b):
        for d in range(2):
            for p in range(2):
                @pl.when((b >= 1) & ((b < half) | ((b == half) & (k == d))))
                def _():
                    zb(d, p, b, back=1).wait_recv()

                @pl.when((b >= 1) & ((b < half - 1) | ((b == half - 1) & (k == d))))
                def _():
                    zb(d, p, b).start()

    @pl.loop(1, half + 3)
    def _(s):
        for d in range(2):
            @pl.when((s < half) | ((s == half) & (k == d)))
            def _():
                zl_in(d, s).wait_recv()

                @pl.when((s < half - 1) | ((s == half - 1) & (k == d)))
                def _():
                    zl(d, s).start()

                yf(d, s).start()
                ce(d, s).start()

        s1 = s - 1
        for d in range(2):
            @pl.when(
                ((s1 == 0) & (d == 0)) | ((s1 >= 1) & (s1 < half)) | ((s1 == half) & (k == d))
            )
            def _():
                yf_in(d, s1).wait_recv()
                co(d, s1).start()

        s2 = s - 2
        for d in range(2):
            there = ((s2 >= 1) & (s2 < half)) | ((s2 == half) & (k == 1 - d))

            @pl.when(there)
            def _():
                ce_in(d, s2).wait_recv()

            @pl.when(there | ((s2 == 0) & (d == 0)))
            def _():
                co_in(d, s2).wait_recv()

        @pl.loop(0, 2)
        def _(d):
            c = jnp.where(d == 0, z - s2, z + s2 - nz)

            @pl.when((s2 >= 0) & (c >= 0) & ((d == 0) | ((s2 >= 1) & (s2 < half))))
            def _():
                attend(c)

        for d in range(2):
            @pl.when((s < half) | ((s == half) & (k == d)))
            def _():
                za(d, s, back=1).wait_recv()

                @pl.when((s < half - 1) | ((s == half - 1) & (k == d)))
                def _():
                    za(d, s).start()

        b = s - (half - 1)

        @pl.when(b == 0)
        def _():
            for d in range(2):
                for p in range(2):
                    zb(d, p, 0, w_ref.at[1, pl.ds(p * sub, sub)]).start()

        relay_b(b)

    for h in range(heads):
        rows = pl.ds(h * tok, tok)
        context = (acc[rows, :] / l_s[rows, :]).astype(jnp.bfloat16)
        vx[yl, :, h * vd:(h + 1) * vd] = jnp.dot(
            context, up_ref[h], preferred_element_type=jnp.float32
        ).astype(jnp.bfloat16)

    rc(vx.at[yl], vx.at[yl], v_s, v_r, ypair).start()
    relay_b(jnp.int32(4))
    rc(vx.at[1 - yl], vx.at[1 - yl], v_s, v_r, ypair).wait_recv()

    def block_of(g, j):
        ab = g // n_a
        i = (g % n_a) * GROUP + j
        off = jnp.where(i % 2 == 1, nz - (i + 1) // 2, i // 2)
        return ab, jnp.where(ab == 0, i, (z + off) % nz)

    def c_copy(g):
        return rc(ps.at[g, 1 - k], cr.at[g], c_s.at[g], c_r.at[g], core)

    def x_copy(g, dx):
        at, to = xn[dx]
        return rc(xs.at[g, at], xr.at[g, dx], x_s.at[g, dx], x_r.at[g, dx], to)

    def y_copy(g, dy):
        at, to = y4[dy]
        return rc(ys.at[g, at], yr.at[g, dy], y_s.at[g, dy], y_r.at[g, dy], to)

    def part(g):
        for j in range(GROUP):
            ab, c = block_of(g, j)
            both = vx[...].reshape(2 * tok, vx.shape[2])
            o = lax.dot_general(
                both, wab[ab, c], (((1,), (1,)), ((), ())), preferred_element_type=jnp.float32
            )
            o = o.reshape(2, tok // 16, 2, 8, LANES)
            for kk in range(2):
                piece = jnp.concatenate([o[0, :, kk], o[1, :, kk]], axis=1)
                ps[g, kk, :, j] = piece.astype(jnp.bfloat16)
        c_copy(g).start()

    def sum_cores(g):
        c_copy(g).wait_recv()
        s = ps[g, k].astype(jnp.float32) + cr[g].astype(jnp.float32)
        s = s.astype(jnp.bfloat16)
        for hi in range(2):
            xs[g, :, hi] = s[hi * nx:(hi + 1) * nx]
        for dx in range(nx - 1):
            x_copy(g, dx).start()

    def sum_x(g):
        t = xs[g, x].astype(jnp.float32)
        for dx in range(nx - 1):
            x_copy(g, dx).wait_recv()
            t = t + xr[g, dx].astype(jnp.float32)
        for hi in range(2):
            for lo in range(2):
                ys[g, hi * 2 + lo] = t[hi, :, lo * 8:(lo + 1) * 8]
        for dy in range(3):
            y_copy(g, dy).start()

    def sum_y(g):
        for dy in range(3):
            y_copy(g, dy).wait_recv()
        own = ys[g, y] + yr[g, 1]
        other = yr[g, 0] + yr[g, 2]
        for j in range(GROUP):
            ab, c = block_of(g, j)
            out_ref[ab, 2 * c + yl] = own[j]
            out_ref[ab, 2 * c + 1 - yl] = other[j]

    @pl.loop(0, n_groups + 3)
    def _(i):
        @pl.when(i % 2 == 1)
        def _():
            relay_b(5 + (i - 1) // 2)

        @pl.when(i < n_groups)
        def _():
            part(i)

        @pl.when((i >= 1) & (i < n_groups + 1))
        def _():
            sum_cores(i - 1)

        @pl.when((i >= 2) & (i < n_groups + 2))
        def _():
            sum_x(i - 2)

        @pl.when(i >= 3)
        def _():
            sum_y(i - 3)

    @pl.loop(0, half + 1)
    def _(s):
        for d in range(2):
            @pl.when((s < half - 1) | ((s == half - 1) & (k == d)))
            def _():
                zl(d, s).wait_send()
                za(d, s).wait_send()
                for p in range(2):
                    zb(d, p, s).wait_send()

            got = ((s >= 1) & (s < half)) | ((s == half) & (k == d))

            @pl.when(got)
            def _():
                ce(d, s).wait_send()

            @pl.when(got | ((s == 0) & (d == 0)))
            def _():
                yf(d, s).wait_send()
                co(d, s).wait_send()

    rc(vx.at[yl], vx.at[yl], v_s, v_r, ypair).wait_send()

    @pl.loop(0, n_groups)
    def _(g):
        c_copy(g).wait_send()
        for dx in range(nx - 1):
            x_copy(g, dx).wait_send()
        for dy in range(3):
            y_copy(g, dy).wait_send()


def shards(queries, latents, value_up, out_weight):
    nz = lax.axis_size("ctx") // 2
    nx = lax.axis_size("exp") // 4
    tok, heads, lat = queries.shape
    nvl, vd = value_up.shape[1], value_up.shape[2]
    rows = tok * heads
    width = heads * vd
    ncol = out_weight.shape[1]
    nb = ncol - LANES
    half = nz // 2
    ng = 2 * (nz // GROUP)
    q = jnp.moveaxis(queries, 1, 0).reshape(rows, lat)
    w = jnp.pad(out_weight.T, ((0, 2 * LANES - ncol), (0, 0))).reshape(2, LANES, width)
    bf, f32 = jnp.bfloat16, jnp.float32
    dma = pltpu.SemaphoreType.DMA
    vmem = pl.BlockSpec(memory_space=pltpu.VMEM)
    out = pl.pallas_call(
        functools.partial(kernel, nz, nx, nvl, nb),
        out_shape=jax.ShapeDtypeStruct((2, 2 * nz, 8, LANES), f32),
        in_specs=[vmem] * 4,
        out_specs=vmem,
        scratch_shapes=[
            pltpu.VMEM((nz, 2 * tok, lat), bf),
            pltpu.VMEM((2, nz, LANES, width), bf),
            pltpu.VMEM((rows, 1), f32),
            pltpu.VMEM((rows, 1), f32),
            pltpu.VMEM((rows, nvl), f32),
            pltpu.VMEM((2, tok, width), bf),
            pltpu.VMEM((ng, 2, 2 * nx, GROUP, 16, LANES), bf),
            pltpu.VMEM((ng, 2 * nx, GROUP, 16, LANES), bf),
            pltpu.VMEM((ng, nx, 2, GROUP, 16, LANES), bf),
            pltpu.VMEM((ng, nx - 1, 2, GROUP, 16, LANES), bf),
            pltpu.VMEM((ng, 4, GROUP, 8, LANES), f32),
            pltpu.VMEM((ng, 3, GROUP, 8, LANES), f32),
        ]
        + [dma((2, half + 1))] * 8
        + [dma((2, half))] * 2
        + [dma((2, 2, half))] * 2
        + [dma(())] * 2
        + [dma((ng,))] * 2
        + [dma((ng, nx - 1))] * 2
        + [dma((ng, 3))] * 2,
        compiler_params=pltpu.CompilerParams(
            collective_id=0, has_side_effects=True, vmem_limit_bytes=56 * 2**20
        ),
        name="latent_attention",
    )(q, latents, value_up, w)
    cols = jnp.concatenate([out[0], out[1, :, :, :nb]], axis=2)
    return jnp.moveaxis(cols, 1, 0).reshape(8, 2 * nz * ncol).astype(bf)


def solution(mesh):
    in_specs = (P("ctx", "exp", None), P("ctx", None), P("exp", None, None), P("exp", "ctx"))
    out_specs = P(("ctx", "exp"), None)
    return jax.shard_map(shards, mesh=mesh, in_specs=in_specs, out_specs=out_specs, check_vma=False)
```

```python
import functools

import jax
import jax.numpy as jnp
from jax import lax
from jax.experimental import pallas as pl
from jax.experimental.pallas import tpu as pltpu
from jax.sharding import PartitionSpec as P

MESH = pl.DeviceIdType.MESH
PIECE = 32
RELAYS = 3
LOG2E = 1.4426950408889634
score_scale = 192.0 ** (-0.5)
LOW = -1e30


def kernel(
    nz, nx, nvl,
    q_ref, lat_ref, up_ref, w_ref, out_ref,
    q_s, lat_s, wab, m_s, l_s, acc, vx, ps, cr, xs, xr, ys, yr,
    zl_s, zl_r, xl_s, xl_r, yf_s, yf_r, ce_s, ce_r, co_s, co_r,
    zw_s, zw_r, v_s, v_r, c_s, c_r, x_s, x_r, y_s, y_r,
):
    half = nz // 2
    lat, tok = lat_ref.shape
    hrow, prow = lat // 2, lat // 4
    heads, _, vd = up_ref.shape
    ncol = w_ref.shape[0]
    pieces = ncol // PIECE

    ctx, ex = lax.axis_index("ctx"), lax.axis_index("exp")
    z, yl = ctx // 2, ctx % 2
    yh, x, k = ex // (2 * nx), (ex // 2) % nx, ex % 2
    y = yh * 2 + yl

    def dev(zz=z, yy=y, xx=x, kk=k):
        return {"ctx": zz * 2 + yy % 2, "exp": (yy // 2) * (2 * nx) + xx * 2 + kk}

    zn = (dev(zz=(z + 1) % nz), dev(zz=(z + nz - 1) % nz))
    yn = (dev(yy=(y + 1) % 4), dev(yy=(y + 3) % 4))
    xl_to = (dev(xx=(x + 1) % nx), dev(xx=(x + nx - 1) % nx))
    core = dev(kk=1 - k)
    ypair = dev(yy=yh * 2 + 1 - yl)
    xn = tuple(((x + dx) % nx, dev(xx=(x + dx) % nx)) for dx in range(1, nx))
    y4 = tuple(((y + dy) % 4, dev(yy=(y + dy) % 4)) for dy in range(1, 4))

    def rc(src, dst, ss, rs, to):
        return pltpu.make_async_remote_copy(
            src_ref=src, dst_ref=dst, send_sem=ss, recv_sem=rs, device_id=to, device_id_type=MESH
        )

    def zc(d, s):
        return (z + nz - s) % nz if d == 0 else (z + s) % nz

    def reaches(s, d):
        return (s < half) | ((s == half) & (k == d))

    def lanes(yy):
        return pl.ds(pl.multiple_of(yy * tok, tok), tok)

    half_rows = pl.ds(pl.multiple_of(k * hrow, hrow), hrow)
    other_rows = pl.ds(pl.multiple_of((1 - k) * hrow, hrow), hrow)
    part_rows = pl.ds(pl.multiple_of(k * hrow + (x % 2) * prow, prow), prow)
    missing_rows = pl.ds(pl.multiple_of(k * hrow + (1 - x % 2) * prow, prow), prow)

    def zl(d, s, src=None, back=0):
        at = lat_s.at[zc(d, s), part_rows, lanes(yl)]
        return rc(at if src is None else src, at, zl_s.at[d, s - back], zl_r.at[d, s - back], zn[d])

    def xl(d, s, rows):
        at = lat_s.at[zc(d, s), rows, lanes(yl)]
        return rc(at, at, xl_s.at[d, s], xl_r.at[d, s], xl_to[d])

    def yf(d, s, yy, src=None):
        at = lat_s.at[zc(d, s), half_rows, lanes(yy)]
        return rc(at if src is None else src, at, yf_s.at[d, s], yf_r.at[d, s], yn[d])

    def ce(d, s, rows):
        at = lat_s.at[zc(d, s), rows, lanes(yl)]
        return rc(at, at, ce_s.at[d, s], ce_r.at[d, s], core)

    def co(d, s, rows):
        at = lat_s.at[zc(d, s), rows, lanes(1 - yl)]
        return rc(at, at, co_s.at[d, s], co_r.at[d, s], core)

    def zw(d, n, back=0, own=False):
        rows = pl.ds(pl.multiple_of((n % pieces) * PIECE, PIECE), PIECE)
        at = wab.at[zc(d, n // pieces), rows]
        m = n - back
        return rc(w_ref.at[rows] if own else at, at, zw_s.at[d, m], zw_r.at[d, m], zn[d])

    def relay(n):
        s = n // pieces
        for d in range(2):
            @pl.when((s >= 1) & reaches(s, d))
            def _():
                zw(d, n, back=pieces).wait_recv()

        for d in range(2):
            @pl.when((n >= 2) & reaches((n - 2) // pieces + 1, d))
            def _():
                zw(d, n - 2).wait_send()

            @pl.when((s >= 1) & reaches(s + 1, d))
            def _():
                zw(d, n).start()

            @pl.when(s == 0)
            def _():
                zw(d, n, own=True).start()

    barrier = pltpu.get_barrier_semaphore()
    peers = [zn[0], zn[1], core] + [t for _, t in xn] + [t for _, t in y4]
    for peer in peers:
        pl.semaphore_signal(barrier, inc=1, device_id=peer, device_id_type=MESH)
    pl.semaphore_wait(barrier, len(peers))

    for d in range(2):
        zl(d, 0, lat_ref.at[part_rows]).start()
    yf(0, 0, yl, lat_ref.at[half_rows]).start()
    for n in range(RELAYS):
        relay(jnp.int32(n))

    for side in range(2):
        @pl.when(yl == side)
        def _():
            lat_s[z, :, side * tok:(side + 1) * tok] = lat_ref[...]
    wab[z] = w_ref[...]
    eye = (
        lax.broadcasted_iota(jnp.int32, (tok, tok), 0)
        == lax.broadcasted_iota(jnp.int32, (tok, tok), 1)
    ).astype(jnp.bfloat16)
    for h in range(heads):
        q_s[h * tok:(h + 1) * tok, :] = lax.dot_general(
            eye, q_ref[h], (((1,), (1,)), ((), ())), preferred_element_type=jnp.float32
        ).astype(jnp.bfloat16)
    m_s[...] = jnp.full_like(m_s, LOW)
    l_s[...] = jnp.zeros_like(l_s)
    acc[...] = jnp.zeros_like(acc)

    def attend(c):
        scores = jnp.dot(
            q_s[...], lat_s[c], preferred_element_type=jnp.float32
        ) * (score_scale * LOG2E)
        rows, cols = scores.shape
        row_pos = z * cols + yl * tok + lax.broadcasted_iota(jnp.int32, (rows, cols), 0) % tok
        key_pos = c * cols + lax.broadcasted_iota(jnp.int32, (rows, cols), 1)
        scores = jnp.where(key_pos <= row_pos, scores, LOW)
        old = m_s[...]
        new = jnp.maximum(old, jnp.max(scores, axis=1, keepdims=True))
        shrink = jnp.exp2(old - new)
        expo = jnp.exp2(scores - new)
        m_s[...] = new
        l_s[...] = l_s[...] * shrink + jnp.sum(expo, axis=1, keepdims=True)
        acc[...] = acc[...] * shrink + lax.dot_general(
            expo.astype(jnp.bfloat16), lat_s[c, :nvl], (((1,), (1,)), ((), ())),
            preferred_element_type=jnp.float32,
        )

    steps = half + 3

    @pl.loop(1, steps + 1)
    def _(s):
        for d in range(2):
            @pl.when(reaches(s, d))
            def _():
                zl(d, s, back=1).wait_recv()

                @pl.when(reaches(s + 1, d))
                def _():
                    zl(d, s).start()

                xl(d, s, part_rows).start()

        relay(RELAYS * s)

        s1 = s - 1
        for d in range(2):
            @pl.when((s1 >= 1) & reaches(s1, d))
            def _():
                xl(d, s1, missing_rows).wait_recv()
                yf(d, s1, yl).start()
                ce(d, s1, half_rows).start()

        s2 = s - 2
        for d in range(2):
            @pl.when(((s2 == 0) & (d == 0)) | ((s2 >= 1) & reaches(s2, d)))
            def _():
                yf(d, s2, 1 - yl).wait_recv()
                co(d, s2, half_rows).start()

        for r in range(1, RELAYS):
            relay(RELAYS * s + r)

        s3 = s - 3
        for d in range(2):
            there = (s3 >= 1) & reaches(s3, 1 - d)

            @pl.when(there)
            def _():
                ce(d, s3, other_rows).wait_recv()

            @pl.when(there | ((s3 == 0) & (d == 0)))
            def _():
                co(d, s3, other_rows).wait_recv()

        @pl.loop(0, 2)
        def _(d):
            c = jnp.where(d == 0, z - s3, z + s3 - nz)

            @pl.when((s3 >= 0) & (c >= 0) & ((d == 0) | ((s3 >= 1) & (s3 < half))))
            def _():
                attend(c)

    for h in range(heads):
        rows = pl.ds(h * tok, tok)
        context = (acc[rows, :] / l_s[rows, :]).astype(jnp.bfloat16)
        vx[yl, :, h * vd:(h + 1) * vd] = jnp.dot(
            context, up_ref[h], preferred_element_type=jnp.float32
        ).astype(jnp.bfloat16)

    rc(vx.at[yl], vx.at[yl], v_s, v_r, ypair).start()
    rc(vx.at[1 - yl], vx.at[1 - yl], v_s, v_r, ypair).wait_recv()

    def block_of(g, j):
        far = g == half - 1
        return zc(0, jnp.where(far, 0, g + 1)) if j == 0 else zc(1, jnp.where(far, half, g + 1))

    def c_copy(g):
        return rc(ps.at[g, 1 - k], cr.at[g], c_s.at[g], c_r.at[g], core)

    def x_copy(g, dx):
        at, to = xn[dx]
        return rc(xs.at[g, at], xr.at[g, dx], x_s.at[g, dx], x_r.at[g, dx], to)

    def y_copy(g, dy):
        at, to = y4[dy]
        return rc(ys.at[g, at], yr.at[g, dy], y_s.at[g, dy], y_r.at[g, dy], to)

    def part(g):
        both = vx[...].reshape(2 * tok, vx.shape[2])
        for j in range(2):
            o = lax.dot_general(
                both, wab[block_of(g, j)], (((1,), (1,)), ((), ())),
                preferred_element_type=jnp.float32,
            )
            o = o.reshape(2, tok // 16, 2, 8, ncol)
            for kk in range(2):
                piece = jnp.concatenate([o[0, :, kk], o[1, :, kk]], axis=1)
                ps[g, kk, :, j] = piece.astype(jnp.bfloat16)
        c_copy(g).start()

    def sum_cores(g):
        c_copy(g).wait_recv()
        s = ps[g, k].astype(jnp.float32) + cr[g].astype(jnp.float32)
        s = s.astype(jnp.bfloat16)
        for hi in range(2):
            xs[g, :, hi] = s[hi * nx:(hi + 1) * nx]
        for dx in range(nx - 1):
            x_copy(g, dx).start()

    def sum_x(g):
        t = xs[g, x].astype(jnp.float32)
        for dx in range(nx - 1):
            x_copy(g, dx).wait_recv()
            t = t + xr[g, dx].astype(jnp.float32)
        for hi in range(2):
            for lo in range(2):
                ys[g, hi * 2 + lo] = t[hi, :, lo * 8:(lo + 1) * 8]
        for dy in range(3):
            y_copy(g, dy).start()

    def sum_y(g):
        for dy in range(3):
            y_copy(g, dy).wait_recv()
        own = (ys[g, y] + yr[g, 1]).astype(out_ref.dtype)
        other = (yr[g, 0] + yr[g, 2]).astype(out_ref.dtype)
        for j in range(2):
            c = block_of(g, j)
            out_ref[2 * c + yl] = own[j]
            out_ref[2 * c + 1 - yl] = other[j]

    done = RELAYS * (steps + 1)
    last = half * pieces + pieces - 1
    first = max(0, min(half, done // pieces - 1))
    late = half - first
    begin = max((first + 1) * pieces + pieces - 1 - done, first)
    gap = max(first, 3)
    stages = (part, sum_cores, sum_x, sum_y)
    ticks = max(last - done + 1, 4 * first, begin + 3 * gap + (late - 1) * pieces + 1 if late else 0)

    @pl.loop(0, ticks)
    def _(t):
        @pl.when(t + done <= last)
        def _():
            relay(t + done)

        for i, stage in enumerate(stages):
            u = t - begin - i * gap
            early = (t >= i * first) & (t < (i + 1) * first)
            after = (u >= 0) & (u % pieces == 0) & (u < late * pieces)

            @pl.when(early | after)
            def _():
                stage(jnp.where(early, t - i * first, first + u // pieces))

    @pl.loop(0, half + 1)
    def _(s):
        for d in range(2):
            @pl.when(reaches(s + 1, d))
            def _():
                zl(d, s).wait_send()

            got = (s >= 1) & reaches(s, d)

            @pl.when(got)
            def _():
                xl(d, s, part_rows).wait_send()
                ce(d, s, half_rows).wait_send()

            @pl.when(got | ((s == 0) & (d == 0)))
            def _():
                yf(d, s, yl).wait_send()
                co(d, s, half_rows).wait_send()

    rc(vx.at[yl], vx.at[yl], v_s, v_r, ypair).wait_send()

    @pl.loop(0, half)
    def _(g):
        c_copy(g).wait_send()
        for dx in range(nx - 1):
            x_copy(g, dx).wait_send()
        for dy in range(3):
            y_copy(g, dy).wait_send()


def shards(queries, latents, value_up, out_weight):
    nz = lax.axis_size("ctx") // 2
    nx = lax.axis_size("exp") // 4
    tok, heads, lat = queries.shape
    nvl, vd = value_up.shape[1], value_up.shape[2]
    rows = tok * heads
    width = heads * vd
    ncol = out_weight.shape[1]
    half = nz // 2
    ng = half
    bf, f32 = jnp.bfloat16, jnp.float32
    dma = pltpu.SemaphoreType.DMA
    vmem = pl.BlockSpec(memory_space=pltpu.VMEM)
    out = pl.pallas_call(
        functools.partial(kernel, nz, nx, nvl),
        out_shape=jax.ShapeDtypeStruct((2 * nz, 8, ncol), bf),
        in_specs=[vmem] * 4,
        out_specs=vmem,
        scratch_shapes=[
            pltpu.VMEM((rows, lat), bf),
            pltpu.VMEM((nz, lat, 2 * tok), bf),
            pltpu.VMEM((nz, ncol, width), bf),
            pltpu.VMEM((rows, 1), f32),
            pltpu.VMEM((rows, 1), f32),
            pltpu.VMEM((rows, nvl), f32),
            pltpu.VMEM((2, tok, width), bf),
            pltpu.VMEM((ng, 2, 2 * nx, 2, 16, ncol), bf),
            pltpu.VMEM((ng, 2 * nx, 2, 16, ncol), bf),
            pltpu.VMEM((ng, nx, 2, 2, 16, ncol), bf),
            pltpu.VMEM((ng, nx - 1, 2, 2, 16, ncol), bf),
            pltpu.VMEM((ng, 4, 2, 8, ncol), f32),
            pltpu.VMEM((ng, 3, 2, 8, ncol), f32),
        ]
        + [dma((2, half + 1))] * 10
        + [dma((2, half * (ncol // PIECE)))] * 2
        + [dma(())] * 2
        + [dma((ng,))] * 2
        + [dma((ng, nx - 1))] * 2
        + [dma((ng, 3))] * 2,
        compiler_params=pltpu.CompilerParams(
            collective_id=0, has_side_effects=True, vmem_limit_bytes=56 * 2**20
        ),
        name="latent_attention",
    )(jnp.transpose(queries, (1, 2, 0)), latents.T, value_up, out_weight.T)
    return jnp.moveaxis(out, 1, 0).reshape(8, 2 * nz * ncol)


def solution(mesh):
    in_specs = (P("ctx", "exp", None), P("ctx", None), P("exp", None, None), P("exp", "ctx"))
    out_specs = P(("ctx", "exp"), None)
    return jax.shard_map(shards, mesh=mesh, in_specs=in_specs, out_specs=out_specs, check_vma=False)
```

```python
import functools

import jax
import jax.numpy as jnp
from jax import lax
from jax.experimental import pallas as pl
from jax.experimental.pallas import tpu as pltpu
from jax.sharding import PartitionSpec as P

MESH = pl.DeviceIdType.MESH
PIECE = 32
RELAYS = 3
FLIGHT = 4
LOG2E = 1.4426950408889634
score_scale = 192.0 ** (-0.5)
LOW = -1e30


def kernel(
    nz, nx, nvl,
    q_ref, lat_ref, up_ref, w_ref, out_ref,
    q_s, lat_s, wab, m_s, l_s, acc, vx, ps, xr, ts, fr,
    zl_s, zl_r, xl_s, xl_r, yf_s, yf_r, ce_s, ce_r, co_s, co_r,
    zw_s, zw_r, zf_s, zf_r, v_s, v_r, r_s, r_r, f_s, f_r,
):
    half = nz // 2
    lat, tok = lat_ref.shape
    hrow, prow = lat // 2, lat // 4
    heads, _, vd = up_ref.shape
    ncol, width = w_ref.shape
    pieces = ncol // PIECE

    ctx, ex = lax.axis_index("ctx"), lax.axis_index("exp")
    z, yl = ctx // 2, ctx % 2
    yh, x, k = ex // (2 * nx), (ex // 2) % nx, ex % 2
    y = yh * 2 + yl

    def dev(zz=z, yy=y, xx=x, kk=k):
        return {"ctx": zz * 2 + yy % 2, "exp": (yy // 2) * (2 * nx) + xx * 2 + kk}

    zn = (dev(zz=(z + 1) % nz), dev(zz=(z + nz - 1) % nz))
    yn = (dev(yy=(y + 1) % 4), dev(yy=(y + 3) % 4))
    xl_to = (dev(xx=(x + 1) % nx), dev(xx=(x + nx - 1) % nx))
    core = dev(kk=1 - k)
    ypair = dev(yy=yh * 2 + 1 - yl)
    ypair_core = dev(yy=yh * 2 + 1 - yl, kk=1 - k)
    plane = tuple(
        ((y + dy) % 4, (x + dx) % nx, dev(yy=(y + dy) % 4, xx=(x + dx) % nx))
        for dy in range(4) for dx in range(nx) if dy or dx
    )

    def rc(src, dst, ss, rs, to):
        return pltpu.make_async_remote_copy(
            src_ref=src, dst_ref=dst, send_sem=ss, recv_sem=rs, device_id=to, device_id_type=MESH
        )

    def zc(d, s):
        return (z + nz - s) % nz if d == 0 else (z + s) % nz

    def reaches(s, d):
        return (s < half) | ((s == half) & (k == d))

    def lanes(yy):
        return pl.ds(pl.multiple_of(yy * tok, tok), tok)

    half_rows = pl.ds(pl.multiple_of(k * hrow, hrow), hrow)
    other_rows = pl.ds(pl.multiple_of((1 - k) * hrow, hrow), hrow)
    part_rows = pl.ds(pl.multiple_of(k * hrow + (x % 2) * prow, prow), prow)
    missing_rows = pl.ds(pl.multiple_of(k * hrow + (1 - x % 2) * prow, prow), prow)

    def zl(d, s, src=None, back=0):
        at = lat_s.at[zc(d, s), part_rows, lanes(yl)]
        return rc(at if src is None else src, at, zl_s.at[d, s - back], zl_r.at[d, s - back], zn[d])

    def xl(d, s, rows):
        at = lat_s.at[zc(d, s), rows, lanes(yl)]
        return rc(at, at, xl_s.at[d, s], xl_r.at[d, s], xl_to[d])

    def yf(d, s, yy, src=None):
        at = lat_s.at[zc(d, s), half_rows, lanes(yy)]
        return rc(at if src is None else src, at, yf_s.at[d, s], yf_r.at[d, s], yn[d])

    def ce(d, s, rows):
        at = lat_s.at[zc(d, s), rows, lanes(yl)]
        return rc(at, at, ce_s.at[d, s], ce_r.at[d, s], core)

    def co(d, s, rows):
        at = lat_s.at[zc(d, s), rows, lanes(1 - yl)]
        return rc(at, at, co_s.at[d, s], co_r.at[d, s], core)

    def wlanes(kk):
        return pl.ds(pl.multiple_of(kk * width, width), width)

    def zf(c, n, own=False):
        rows = pl.ds(pl.multiple_of((n % pieces) * PIECE, PIECE), PIECE)
        at = wab.at[c, rows, wlanes(k)]
        s = n // pieces
        return rc(w_ref.at[rows] if own else at, at, zf_s.at[s], zf_r.at[s], core)

    def zf_block(c, s, kk):
        at = wab.at[c, :, wlanes(kk)]
        return rc(at, at, zf_s.at[s], zf_r.at[s], core)

    def zw(d, n, back=0, own=False):
        rows = pl.ds(pl.multiple_of((n % pieces) * PIECE, PIECE), PIECE)
        at = wab.at[zc(d, n // pieces), rows, wlanes(k)]
        m = n - back
        return rc(w_ref.at[rows] if own else at, at, zw_s.at[d, m], zw_r.at[d, m], zn[d])

    def relay(n):
        s = n // pieces
        for d in range(2):
            @pl.when((s >= 1) & reaches(s, d))
            def _():
                zw(d, n, back=pieces).wait_recv()

                @pl.when(((s < half) & (k != d)) | ((s == half) & (k == 0)))
                def _():
                    zf(zc(d, s), n).start()

        @pl.when((s == 0) & (k == 1))
        def _():
            zf(z, n, own=True).start()

        for d in range(2):
            @pl.when((n >= FLIGHT) & reaches((n - FLIGHT) // pieces + 1, d))
            def _():
                zw(d, n - FLIGHT).wait_send()

            @pl.when((s >= 1) & reaches(s + 1, d))
            def _():
                zw(d, n).start()

            @pl.when(s == 0)
            def _():
                zw(d, n, own=True).start()

    barrier = pltpu.get_barrier_semaphore()
    peers = [zn[0], zn[1], core, ypair_core] + [t for _, _, t in plane]
    for peer in peers:
        pl.semaphore_signal(barrier, inc=1, device_id=peer, device_id_type=MESH)
    pl.semaphore_wait(barrier, len(peers))

    for d in range(2):
        zl(d, 0, lat_ref.at[part_rows]).start()
    yf(0, 0, yl, lat_ref.at[half_rows]).start()
    for n in range(RELAYS):
        relay(jnp.int32(n))

    for side in range(2):
        @pl.when(yl == side)
        def _():
            lat_s[z, :, side * tok:(side + 1) * tok] = lat_ref[...]
    for side in range(2):
        @pl.when(k == side)
        def _():
            wab[z, :, side * width:(side + 1) * width] = w_ref[...]
    eye = (
        lax.broadcasted_iota(jnp.int32, (tok, tok), 0)
        == lax.broadcasted_iota(jnp.int32, (tok, tok), 1)
    ).astype(jnp.bfloat16)
    for h in range(heads):
        q_s[h * tok:(h + 1) * tok, :] = lax.dot_general(
            eye, q_ref[h], (((1,), (1,)), ((), ())), preferred_element_type=jnp.float32
        ).astype(jnp.bfloat16)
    m_s[...] = jnp.full_like(m_s, LOW)
    l_s[...] = jnp.zeros_like(l_s)
    acc[...] = jnp.zeros_like(acc)

    def attend(c):
        scores = jnp.dot(
            q_s[...], lat_s[c], preferred_element_type=jnp.float32
        ) * (score_scale * LOG2E)
        rows, cols = scores.shape
        row_pos = z * cols + yl * tok + lax.broadcasted_iota(jnp.int32, (rows, cols), 0) % tok
        key_pos = c * cols + lax.broadcasted_iota(jnp.int32, (rows, cols), 1)
        scores = jnp.where(key_pos <= row_pos, scores, LOW)
        old = m_s[...]
        new = jnp.maximum(old, jnp.max(scores, axis=1, keepdims=True))
        shrink = jnp.exp2(old - new)
        expo = jnp.exp2(scores - new)
        m_s[...] = new
        l_s[...] = l_s[...] * shrink + jnp.sum(expo, axis=1, keepdims=True)
        acc[...] = acc[...] * shrink + lax.dot_general(
            expo.astype(jnp.bfloat16), lat_s[c, :nvl], (((1,), (1,)), ((), ())),
            preferred_element_type=jnp.float32,
        )

    steps = half + 3

    @pl.loop(1, steps + 1)
    def _(s):
        for d in range(2):
            @pl.when(reaches(s, d))
            def _():
                zl(d, s, back=1).wait_recv()

                @pl.when(reaches(s + 1, d))
                def _():
                    zl(d, s).start()

                xl(d, s, part_rows).start()

        relay(RELAYS * s)

        s1 = s - 1
        for d in range(2):
            @pl.when((s1 >= 1) & reaches(s1, d))
            def _():
                xl(d, s1, missing_rows).wait_recv()
                yf(d, s1, yl).start()
                ce(d, s1, half_rows).start()

        s2 = s - 2
        for d in range(2):
            @pl.when(((s2 == 0) & (d == 0)) | ((s2 >= 1) & reaches(s2, d)))
            def _():
                yf(d, s2, 1 - yl).wait_recv()
                co(d, s2, half_rows).start()

        for r in range(1, RELAYS - 1):
            relay(RELAYS * s + r)

        s3 = s - 3
        for d in range(2):
            there = (s3 >= 1) & reaches(s3, 1 - d)

            @pl.when(there)
            def _():
                ce(d, s3, other_rows).wait_recv()

            @pl.when(there | ((s3 == 0) & (d == 0)))
            def _():
                co(d, s3, other_rows).wait_recv()

        @pl.loop(0, 2)
        def _(d):
            c = jnp.where(d == 0, z - s3, z + s3 - nz)

            @pl.when((s3 >= 0) & (c >= 0) & ((d == 0) | ((s3 >= 1) & (s3 < half))))
            def _():
                attend(c)

            @pl.when(d == 0)
            def _():
                relay(RELAYS * s + RELAYS - 1)

    made = []
    for h in range(heads):
        rows = pl.ds(h * tok, tok)
        context = (acc[rows, :] / l_s[rows, :]).astype(jnp.bfloat16)
        made.append(
            jnp.dot(context, up_ref[h], preferred_element_type=jnp.float32).astype(jnp.bfloat16)
        )
    made = jnp.concatenate(made, axis=1)
    for side in range(2):
        @pl.when(k == side)
        def _():
            vx[yl, :, side * width:(side + 1) * width] = made

    def v_copy(i, yy, kk):
        at = vx.at[yy, :, wlanes(kk)]
        return rc(at, at, v_s.at[i], v_r.at[i], (core, ypair, ypair_core)[i])

    for i in range(3):
        v_copy(i, yl, k).start()
    v_copy(0, yl, 1 - k).wait_recv()
    v_copy(1, 1 - yl, k).wait_recv()
    v_copy(2, 1 - yl, 1 - k).wait_recv()

    def steps_of(g, kk):
        return g + kk

    def block_of(g, kk):
        return jnp.where(kk == 0, zc(0, g), zc(1, g + 1))

    def f_copy(g):
        return rc(ts.at[g, 1 - k], fr.at[g], f_s.at[g], f_r.at[g], core)

    def r_all(g):
        return rc(xr.at[g], xr.at[g], r_s.at[g], r_r.at[g], core)

    def part(g):
        c = block_of(g, k)
        zf_block(c, steps_of(g, k), 1 - k).wait_recv()
        o = lax.dot_general(
            vx[...].reshape(2 * tok, 2 * width), wab[c], (((1,), (1,)), ((), ())),
            preferred_element_type=jnp.float32,
        ).astype(jnp.bfloat16)
        o = o.reshape(2, 2, nx, 16, ncol)
        for hi in range(2):
            for lo in range(2):
                ps[g, hi * 2 + lo] = o[lo, hi]
        for i, (yy, xx, to) in enumerate(plane):
            rc(ps.at[g, yy, xx], xr.at[g, i], r_s.at[g], r_r.at[g], to).start()

    def sum_plane(g):
        r_all(g).wait_recv()
        own, other = ps[g, y, x].astype(jnp.float32), None
        for i in range(4 * nx - 1):
            term = xr[g, i].astype(jnp.float32)
            if ((i + 1) // nx) % 2 == 0:
                own = own + term
            else:
                other = term if other is None else other + term
        for side, total in enumerate((own, other)):
            for kk in range(2):
                ts[g, kk, side] = total[kk * 8:(kk + 1) * 8].astype(ts.dtype)
        f_copy(g).start()
        c = block_of(g, k)
        out_ref[2 * c + yl] = ts[g, k, 0]
        out_ref[2 * c + 1 - yl] = ts[g, k, 1]

    def finish(g):
        f_copy(g).wait_recv()
        c = block_of(g, 1 - k)
        out_ref[2 * c + yl] = fr[g, 0]
        out_ref[2 * c + 1 - yl] = fr[g, 1]

    done = RELAYS * (steps + 1)
    last = half * pieces + pieces - 1
    first = max(0, min(half, done // pieces - 1))
    late = half - first
    begin = max((first + 1) * pieces + pieces - 1 - done, first)
    gap = max(first, 3)
    stages = (part, sum_plane, finish)
    ticks = max(last - done + 1, 3 * first, begin + 2 * gap + (late - 1) * pieces + 1 if late else 0)

    @pl.loop(0, ticks)
    def _(t):
        @pl.when(t + done <= last)
        def _():
            relay(t + done)

        for i, stage in enumerate(stages):
            u = t - begin - i * gap
            early = (t >= i * first) & (t < (i + 1) * first)
            after = (u >= 0) & (u % pieces == 0) & (u < late * pieces)

            @pl.when(early | after)
            def _():
                stage(jnp.where(early, t - i * first, first + u // pieces))

    @pl.loop(0, half + 1)
    def _(s):
        for d in range(2):
            @pl.when(reaches(s + 1, d))
            def _():
                zl(d, s).wait_send()

            got = (s >= 1) & reaches(s, d)

            @pl.when(got)
            def _():
                xl(d, s, part_rows).wait_send()
                ce(d, s, half_rows).wait_send()

            @pl.when(got | ((s == 0) & (d == 0)))
            def _():
                yf(d, s, yl).wait_send()
                co(d, s, half_rows).wait_send()

    for i in range(3):
        v_copy(i, yl, k).wait_send()

    @pl.loop(0, half)
    def _(g):
        zf_block(block_of(g, 1 - k), steps_of(g, 1 - k), k).wait_send()
        r_all(g).wait_send()
        f_copy(g).wait_send()


def shards(queries, latents, value_up, out_weight):
    nz = lax.axis_size("ctx") // 2
    nx = lax.axis_size("exp") // 4
    tok, heads, lat = queries.shape
    nvl, vd = value_up.shape[1], value_up.shape[2]
    rows = tok * heads
    width = heads * vd
    ncol = out_weight.shape[1]
    half = nz // 2
    ng = half
    bf, f32 = jnp.bfloat16, jnp.float32
    dma = pltpu.SemaphoreType.DMA
    vmem = pl.BlockSpec(memory_space=pltpu.VMEM)
    out = pl.pallas_call(
        functools.partial(kernel, nz, nx, nvl),
        out_shape=jax.ShapeDtypeStruct((2 * nz, 8, ncol), bf),
        in_specs=[vmem] * 4,
        out_specs=vmem,
        scratch_shapes=[
            pltpu.VMEM((rows, lat), bf),
            pltpu.VMEM((nz, lat, 2 * tok), bf),
            pltpu.VMEM((nz, ncol, 2 * width), bf),
            pltpu.VMEM((rows, 1), f32),
            pltpu.VMEM((rows, 1), f32),
            pltpu.VMEM((rows, nvl), f32),
            pltpu.VMEM((2, tok, 2 * width), bf),
            pltpu.VMEM((ng, 4, nx, 16, ncol), bf),
            pltpu.VMEM((ng, 4 * nx - 1, 16, ncol), bf),
            pltpu.VMEM((ng, 2, 2, 8, ncol), bf),
            pltpu.VMEM((ng, 2, 8, ncol), bf),
        ]
        + [dma((2, half + 1))] * 10
        + [dma((2, half * (ncol // PIECE)))] * 2
        + [dma((half + 1,))] * 2
        + [dma((3,))] * 2
        + [dma((ng,))] * 4,
        compiler_params=pltpu.CompilerParams(
            collective_id=0, has_side_effects=True, vmem_limit_bytes=56 * 2**20
        ),
        name="latent_attention",
    )(jnp.transpose(queries, (1, 2, 0)), latents.T, value_up, out_weight.T)
    return jnp.moveaxis(out, 1, 0).reshape(8, 2 * nz * ncol)


def solution(mesh):
    in_specs = (P("ctx", "exp", None), P("ctx", None), P("exp", None, None), P("exp", "ctx"))
    out_specs = P(("ctx", "exp"), None)
    return jax.shard_map(shards, mesh=mesh, in_specs=in_specs, out_specs=out_specs, check_vma=False)
```

```python
import functools

import jax
import jax.numpy as jnp
from jax import lax
from jax.experimental import pallas as pl
from jax.experimental.pallas import tpu as pltpu
from jax.sharding import PartitionSpec as P

MESH = pl.DeviceIdType.MESH
PIECE = 112
FLIGHT = 2
LOG2E = 1.4426950408889634
score_scale = 192.0 ** (-0.5)
LOW = -1e30


def when(*conditions):
    if any(c is False for c in conditions):
        return lambda body: None
    traced = [c for c in conditions if c is not True]
    if not traced:
        return lambda body: body()
    return pl.when(functools.reduce(lambda a, b: a & b, traced))


def order_of(relays, groups, ready_after):
    pace, exchange, swap = 2.75, 5.5, 1.6
    costs = {"part": 1.0, "sum": 0.5, "end": 0.2, "relay": 0.1}
    now, out, n, p = 0.0, [], 0, 0
    sums, ends = [], []
    while len([o for o in out if o[0] == "end"]) < groups or n < len(relays):
        if n < len(relays) and now >= (n + 1) * pace:
            step = ("relay", relays[n])
            n += 1
        elif p < groups and ready_after[p] <= n:
            step = ("part", p)
            sums.append((now + exchange, p))
            p += 1
        elif sums and now >= sums[0][0]:
            step = ("sum", sums[0][1])
            ends.append((now + swap, sums.pop(0)[1]))
        elif ends and now >= ends[0][0]:
            step = ("end", ends.pop(0)[1])
        else:
            waits = [(n + 1) * pace] * (n < len(relays)) + [q[0] for q in sums[:1] + ends[:1]]
            now = max(now, min(waits)) + 1e-6
            continue
        now += costs[step[0]]
        out.append(step)
    return out


def kernel(
    nz, nx, nvl,
    q_ref, lat_ref, up_ref, w_ref, out_ref,
    q_s, lat_s, wab, m_s, l_s, acc, vx, ps, xr, ts, fr,
    zl_s, zl_r, xl_s, xl_r, yf_s, yf_r, ce_s, ce_r, co_s, co_r,
    zw_s, zw_r, zf_s, zf_r, v_s, v_r, r_s, r_r, f_s, f_r,
):
    half = nz // 2
    lat, tok = lat_ref.shape
    hrow, prow = lat // 2, lat // 4
    heads, _, vd = up_ref.shape
    ncol, width = w_ref.shape
    pieces = ncol // PIECE

    ctx, ex = lax.axis_index("ctx"), lax.axis_index("exp")
    z, yl = ctx // 2, ctx % 2
    yh, x, k = ex // (2 * nx), (ex // 2) % nx, ex % 2
    y = yh * 2 + yl

    def dev(zz=z, yy=y, xx=x, kk=k):
        return {"ctx": zz * 2 + yy % 2, "exp": (yy // 2) * (2 * nx) + xx * 2 + kk}

    zn = (dev(zz=(z + 1) % nz), dev(zz=(z + nz - 1) % nz))
    yn = (dev(yy=(y + 1) % 4), dev(yy=(y + 3) % 4))
    xl_to = (dev(xx=(x + 1) % nx), dev(xx=(x + nx - 1) % nx))
    core = dev(kk=1 - k)
    ypair = dev(yy=yh * 2 + 1 - yl)
    ypair_core = dev(yy=yh * 2 + 1 - yl, kk=1 - k)
    plane = tuple(
        ((y + dy) % 4, (x + dx) % nx, dev(yy=(y + dy) % 4, xx=(x + dx) % nx))
        for dy in range(4) for dx in range(nx) if dy or dx
    )

    def rc(src, dst, ss, rs, to):
        return pltpu.make_async_remote_copy(
            src_ref=src, dst_ref=dst, send_sem=ss, recv_sem=rs, device_id=to, device_id_type=MESH
        )

    def zc(d, s):
        return (z + nz - s) % nz if d == 0 else (z + s) % nz

    def reaches(s, d):
        return True if s < half else (k == d if s == half else False)

    def lanes(yy):
        return pl.ds(pl.multiple_of(yy * tok, tok), tok)

    half_rows = pl.ds(pl.multiple_of(k * hrow, hrow), hrow)
    other_rows = pl.ds(pl.multiple_of((1 - k) * hrow, hrow), hrow)
    part_rows = pl.ds(pl.multiple_of(k * hrow + (x % 2) * prow, prow), prow)
    missing_rows = pl.ds(pl.multiple_of(k * hrow + (1 - x % 2) * prow, prow), prow)

    def zl(d, s, src=None, back=0):
        at = lat_s.at[zc(d, s), part_rows, lanes(yl)]
        return rc(at if src is None else src, at, zl_s.at[d, s - back], zl_r.at[d, s - back], zn[d])

    def xl(d, s, rows):
        at = lat_s.at[zc(d, s), rows, lanes(yl)]
        return rc(at, at, xl_s.at[d, s], xl_r.at[d, s], xl_to[d])

    def yf(d, s, yy, src=None):
        at = lat_s.at[zc(d, s), half_rows, lanes(yy)]
        return rc(at if src is None else src, at, yf_s.at[d, s], yf_r.at[d, s], yn[d])

    def ce(d, s, rows):
        at = lat_s.at[zc(d, s), rows, lanes(yl)]
        return rc(at, at, ce_s.at[d, s], ce_r.at[d, s], core)

    def co(d, s, rows):
        at = lat_s.at[zc(d, s), rows, lanes(1 - yl)]
        return rc(at, at, co_s.at[d, s], co_r.at[d, s], core)

    def wlanes(kk):
        return pl.ds(pl.multiple_of(kk * width, width), width)

    def zf(c, n, own=False):
        rows = pl.ds((n % pieces) * PIECE, PIECE)
        at = wab.at[c, rows, wlanes(k)]
        s = n // pieces
        return rc(w_ref.at[rows] if own else at, at, zf_s.at[s], zf_r.at[s], core)

    def zf_block(c, s, kk):
        at = wab.at[c, :, wlanes(kk)]
        return rc(at, at, zf_s.at[s], zf_r.at[s], core)

    def zw(d, n, back=0, own=False):
        rows = pl.ds((n % pieces) * PIECE, PIECE)
        at = wab.at[zc(d, n // pieces), rows, wlanes(k)]
        m = n - back
        return rc(w_ref.at[rows] if own else at, at, zw_s.at[d, m], zw_r.at[d, m], zn[d])

    def relay(n):
        s = n // pieces
        for d in range(2):
            @when(s >= 1, reaches(s, d))
            def _():
                zw(d, n, back=pieces).wait_recv()

                @pl.when(k != d if s < half else k == 0)
                def _():
                    zf(zc(d, s), n).start()

        @when(s == 0, k == 1)
        def _():
            zf(z, n, own=True).start()

        for d in range(2):
            @when(n >= FLIGHT, reaches((n - FLIGHT) // pieces + 1, d))
            def _():
                zw(d, n - FLIGHT).wait_send()

            @when(reaches(s + 1, d))
            def _():
                zw(d, n, own=s == 0).start()

    barrier = pltpu.get_barrier_semaphore()
    peers = [zn[0], zn[1], core, ypair_core] + [t for _, _, t in plane]
    for peer in peers:
        pl.semaphore_signal(barrier, inc=1, device_id=peer, device_id_type=MESH)
    pl.semaphore_wait(barrier, len(peers))

    for d in range(2):
        zl(d, 0, lat_ref.at[part_rows]).start()
    yf(0, 0, yl, lat_ref.at[half_rows]).start()
    relay(0)

    for side in range(2):
        @pl.when(yl == side)
        def _():
            lat_s[z, :, side * tok:(side + 1) * tok] = lat_ref[...]
    for side in range(2):
        @pl.when(k == side)
        def _():
            wab[z, :, side * width:(side + 1) * width] = w_ref[...]
    eye = (
        lax.broadcasted_iota(jnp.int32, (tok, tok), 0)
        == lax.broadcasted_iota(jnp.int32, (tok, tok), 1)
    ).astype(jnp.bfloat16)
    for h in range(heads):
        q_s[h * tok:(h + 1) * tok, :] = lax.dot_general(
            eye, q_ref[h], (((1,), (1,)), ((), ())), preferred_element_type=jnp.float32
        ).astype(jnp.bfloat16)
    m_s[...] = jnp.full_like(m_s, LOW)
    l_s[...] = jnp.zeros_like(l_s)
    acc[...] = jnp.zeros_like(acc)

    def attend(c, diagonal):
        scores = jnp.dot(
            q_s[...], lat_s[c], preferred_element_type=jnp.float32
        ) * (score_scale * LOG2E)
        if diagonal:
            row_pos = yl * tok + lax.broadcasted_iota(jnp.int32, scores.shape, 0) % tok
            key_pos = lax.broadcasted_iota(jnp.int32, scores.shape, 1)
            scores = jnp.where(key_pos <= row_pos, scores, LOW)
        old = m_s[...]
        new = jnp.maximum(old, jnp.max(scores, axis=1, keepdims=True))
        shrink = jnp.exp2(old - new)
        expo = jnp.exp2(scores - new)
        m_s[...] = new
        l_s[...] = l_s[...] * shrink + jnp.sum(expo, axis=1, keepdims=True)
        acc[...] = acc[...] * shrink + lax.dot_general(
            expo.astype(jnp.bfloat16), lat_s[c, :nvl], (((1,), (1,)), ((), ())),
            preferred_element_type=jnp.float32,
        )

    steps = half + 3

    for s in range(1, steps + 1):
        for d in range(2):
            @when(reaches(s, d))
            def _():
                zl(d, s, back=1).wait_recv()

                @when(reaches(s + 1, d))
                def _():
                    zl(d, s).start()

                xl(d, s, part_rows).start()

        s1 = s - 1
        for d in range(2):
            @when(s1 >= 1, reaches(s1, d))
            def _():
                xl(d, s1, missing_rows).wait_recv()
                yf(d, s1, yl).start()
                ce(d, s1, half_rows).start()

        s2 = s - 2
        for d in range(2):
            @when(s2 >= 1 or (s2 == 0 and d == 0), s2 == 0 or reaches(s2, d))
            def _():
                yf(d, s2, 1 - yl).wait_recv()
                co(d, s2, half_rows).start()

        relay(s)

        s3 = s - 3
        for d in range(2):
            there = reaches(s3, 1 - d)

            @when(s3 >= 1, there)
            def _():
                ce(d, s3, other_rows).wait_recv()

            @when(s3 >= 1 or (s3 == 0 and d == 0), s3 == 0 or there)
            def _():
                co(d, s3, other_rows).wait_recv()

        if s3 == 0:
            attend(z, True)
        if s3 >= 1:
            @pl.loop(0, 2 if s3 < half else 1)
            def _(d):
                c = jnp.where(d == 0, z - s3, z + s3 - nz)

                @pl.when(c >= 0)
                def _():
                    attend(c, False)

    made = []
    for h in range(heads):
        rows = pl.ds(h * tok, tok)
        context = (acc[rows, :] / l_s[rows, :]).astype(jnp.bfloat16)
        made.append(
            jnp.dot(context, up_ref[h], preferred_element_type=jnp.float32).astype(jnp.bfloat16)
        )
    made = jnp.concatenate(made, axis=1)
    for side in range(2):
        @pl.when(k == side)
        def _():
            vx[yl, :, side * width:(side + 1) * width] = made

    def v_copy(i, yy, kk):
        at = vx.at[yy, :, wlanes(kk)]
        return rc(at, at, v_s.at[i], v_r.at[i], (core, ypair, ypair_core)[i])

    for i in range(3):
        v_copy(i, yl, k).start()
    v_copy(0, yl, 1 - k).wait_recv()
    v_copy(1, 1 - yl, k).wait_recv()
    v_copy(2, 1 - yl, 1 - k).wait_recv()

    def steps_of(g, kk):
        return g + kk

    def block_of(g, kk):
        return jnp.where(kk == 0, zc(0, g), zc(1, g + 1))

    def f_copy(g):
        return rc(ts.at[g, 1 - k], fr.at[g], f_s.at[g], f_r.at[g], core)

    def r_all(g):
        return rc(xr.at[g], xr.at[g], r_s.at[g], r_r.at[g], core)

    def part(g):
        c = block_of(g, k)
        zf_block(c, steps_of(g, k), 1 - k).wait_recv()
        o = lax.dot_general(
            vx[...].reshape(2 * tok, 2 * width), wab[c], (((1,), (1,)), ((), ())),
            preferred_element_type=jnp.float32,
        ).astype(jnp.bfloat16)
        o = o.reshape(2, 2, nx, 16, ncol)
        for hi in range(2):
            for lo in range(2):
                ps[g, hi * 2 + lo] = o[lo, hi]
        for i, (yy, xx, to) in enumerate(plane):
            rc(ps.at[g, yy, xx], xr.at[g, i], r_s.at[g], r_r.at[g], to).start()

    def sum_plane(g):
        r_all(g).wait_recv()
        own, other = ps[g, y, x].astype(jnp.float32), None
        for i in range(4 * nx - 1):
            term = xr[g, i].astype(jnp.float32)
            if ((i + 1) // nx) % 2 == 0:
                own = own + term
            else:
                other = term if other is None else other + term
        for side, total in enumerate((own, other)):
            for kk in range(2):
                ts[g, kk, side] = total[kk * 8:(kk + 1) * 8].astype(ts.dtype)
        f_copy(g).start()
        c = block_of(g, k)
        out_ref[2 * c + yl] = ts[g, k, 0]
        out_ref[2 * c + 1 - yl] = ts[g, k, 1]

    def finish(g):
        f_copy(g).wait_recv()
        c = block_of(g, 1 - k)
        out_ref[2 * c + yl] = fr[g, 0]
        out_ref[2 * c + 1 - yl] = fr[g, 1]

    relays = list(range(steps + 1, half * pieces + pieces))
    ready_after = [max(0, (g + 2) * pieces - (steps + 1)) for g in range(half)]
    stages = {"part": part, "sum": sum_plane, "end": finish, "relay": relay}
    for name, index in order_of(relays, half, ready_after):
        stages[name](index)

    for s in range(half + 1):
        for d in range(2):
            @when(reaches(s + 1, d))
            def _():
                zl(d, s).wait_send()

            @when(s >= 1, reaches(s, d))
            def _():
                xl(d, s, part_rows).wait_send()
                ce(d, s, half_rows).wait_send()

            @when(s >= 1 or d == 0, s == 0 or reaches(s, d))
            def _():
                yf(d, s, yl).wait_send()
                co(d, s, half_rows).wait_send()

    for i in range(3):
        v_copy(i, yl, k).wait_send()

    for g in range(half):
        zf_block(block_of(g, 1 - k), steps_of(g, 1 - k), k).wait_send()
        r_all(g).wait_send()
        f_copy(g).wait_send()


def shards(queries, latents, value_up, out_weight):
    nz = lax.axis_size("ctx") // 2
    nx = lax.axis_size("exp") // 4
    tok, heads, lat = queries.shape
    nvl, vd = value_up.shape[1], value_up.shape[2]
    rows = tok * heads
    width = heads * vd
    ncol = out_weight.shape[1]
    half = nz // 2
    ng = half
    bf, f32 = jnp.bfloat16, jnp.float32
    dma = pltpu.SemaphoreType.DMA
    vmem = pl.BlockSpec(memory_space=pltpu.VMEM)
    out = pl.pallas_call(
        functools.partial(kernel, nz, nx, nvl),
        out_shape=jax.ShapeDtypeStruct((2 * nz, 8, ncol), bf),
        in_specs=[vmem] * 4,
        out_specs=vmem,
        scratch_shapes=[
            pltpu.VMEM((rows, lat), bf),
            pltpu.VMEM((nz, lat, 2 * tok), bf),
            pltpu.VMEM((nz, ncol, 2 * width), bf),
            pltpu.VMEM((rows, 1), f32),
            pltpu.VMEM((rows, 1), f32),
            pltpu.VMEM((rows, nvl), f32),
            pltpu.VMEM((2, tok, 2 * width), bf),
            pltpu.VMEM((ng, 4, nx, 16, ncol), bf),
            pltpu.VMEM((ng, 4 * nx - 1, 16, ncol), bf),
            pltpu.VMEM((ng, 2, 2, 8, ncol), bf),
            pltpu.VMEM((ng, 2, 8, ncol), bf),
        ]
        + [dma((2, half + 1))] * 10
        + [dma((2, half * (ncol // PIECE)))] * 2
        + [dma((half + 1,))] * 2
        + [dma((3,))] * 2
        + [dma((ng,))] * 4,
        compiler_params=pltpu.CompilerParams(
            collective_id=0, has_side_effects=True, vmem_limit_bytes=56 * 2**20
        ),
        name="latent_attention",
    )(jnp.transpose(queries, (1, 2, 0)), latents.T, value_up, out_weight.T)
    return jnp.moveaxis(out, 1, 0).reshape(8, 2 * nz * ncol)


def solution(mesh):
    in_specs = (P("ctx", "exp", None), P("ctx", None), P("exp", None, None), P("exp", "ctx"))
    out_specs = P(("ctx", "exp"), None)
    return jax.shard_map(shards, mesh=mesh, in_specs=in_specs, out_specs=out_specs, check_vma=False)
```

```python
import functools

import jax
import jax.numpy as jnp
from jax import lax
from jax.experimental import pallas as pl
from jax.experimental.pallas import tpu as pltpu
from jax.sharding import PartitionSpec as P

MESH = pl.DeviceIdType.MESH
PIECE = 112
EXTRA = (3, 6, 9)
FLIGHT = 2
LOG2E = 1.4426950408889634
score_scale = 192.0 ** (-0.5)
LOW = -1e30


def when(*conditions):
    if any(c is False for c in conditions):
        return lambda body: None
    traced = [c for c in conditions if c is not True]
    if not traced:
        return lambda body: body()
    return pl.when(functools.reduce(lambda a, b: a & b, traced))


def order_of(relays, groups, ready_after):
    pace, exchange, swap = 2.75, 5.5, 1.6
    costs = {"part": 1.0, "sum": 0.5, "end": 0.2, "relay": 0.1}
    now, out, n, p = 0.0, [], 0, 0
    sums, ends = [], []
    while len([o for o in out if o[0] == "end"]) < groups or n < len(relays):
        if n < len(relays) and now >= (n + 1) * pace:
            step = ("relay", relays[n])
            n += 1
        elif p < groups and ready_after[p] <= n:
            step = ("part", p)
            sums.append((now + exchange, p))
            p += 1
        elif sums and now >= sums[0][0]:
            step = ("sum", sums[0][1])
            ends.append((now + swap, sums.pop(0)[1]))
        elif ends and now >= ends[0][0]:
            step = ("end", ends.pop(0)[1])
        else:
            waits = [(n + 1) * pace] * (n < len(relays)) + [q[0] for q in sums[:1] + ends[:1]]
            now = max(now, min(waits)) + 1e-6
            continue
        now += costs[step[0]]
        out.append(step)
    return out


def kernel(
    nz, nx, nvl,
    q_ref, lat_ref, up_ref, w_ref, out_ref,
    q_s, lat_s, wab, m_s, l_s, acc, vx, ps, xr, ts, fr,
    zl_s, zl_r, xl_s, xl_r, yf_s, yf_r, ce_s, ce_r, co_s, co_r,
    zw_s, zw_r, zf_s, zf_r, v_s, v_r, r_s, r_r, f_s, f_r,
):
    half = nz // 2
    lat, tok = lat_ref.shape
    hrow, prow = lat // 2, lat // 4
    heads, _, vd = up_ref.shape
    ncol, width = w_ref.shape
    pieces = ncol // PIECE

    ctx, ex = lax.axis_index("ctx"), lax.axis_index("exp")
    z, yl = ctx // 2, ctx % 2
    yh, x, k = ex // (2 * nx), (ex // 2) % nx, ex % 2
    y = yh * 2 + yl

    def dev(zz=z, yy=y, xx=x, kk=k):
        return {"ctx": zz * 2 + yy % 2, "exp": (yy // 2) * (2 * nx) + xx * 2 + kk}

    zn = (dev(zz=(z + 1) % nz), dev(zz=(z + nz - 1) % nz))
    yn = (dev(yy=(y + 1) % 4), dev(yy=(y + 3) % 4))
    xl_to = (dev(xx=(x + 1) % nx), dev(xx=(x + nx - 1) % nx))
    core = dev(kk=1 - k)
    ypair = dev(yy=yh * 2 + 1 - yl)
    ypair_core = dev(yy=yh * 2 + 1 - yl, kk=1 - k)
    plane = tuple(
        ((y + dy) % 4, (x + dx) % nx, dev(yy=(y + dy) % 4, xx=(x + dx) % nx))
        for dy in range(4) for dx in range(nx) if dy or dx
    )

    def rc(src, dst, ss, rs, to):
        return pltpu.make_async_remote_copy(
            src_ref=src, dst_ref=dst, send_sem=ss, recv_sem=rs, device_id=to, device_id_type=MESH
        )

    def zc(d, s):
        return (z + nz - s) % nz if d == 0 else (z + s) % nz

    def reaches(s, d):
        return True if s < half else (k == d if s == half else False)

    def lanes(yy):
        return pl.ds(pl.multiple_of(yy * tok, tok), tok)

    half_rows = pl.ds(pl.multiple_of(k * hrow, hrow), hrow)
    other_rows = pl.ds(pl.multiple_of((1 - k) * hrow, hrow), hrow)
    part_rows = pl.ds(pl.multiple_of(k * hrow + (x % 2) * prow, prow), prow)
    missing_rows = pl.ds(pl.multiple_of(k * hrow + (1 - x % 2) * prow, prow), prow)

    def zl(d, s, src=None, back=0):
        at = lat_s.at[zc(d, s), part_rows, lanes(yl)]
        return rc(at if src is None else src, at, zl_s.at[d, s - back], zl_r.at[d, s - back], zn[d])

    def xl(d, s, rows):
        at = lat_s.at[zc(d, s), rows, lanes(yl)]
        return rc(at, at, xl_s.at[d, s], xl_r.at[d, s], xl_to[d])

    def yf(d, s, yy, src=None):
        at = lat_s.at[zc(d, s), half_rows, lanes(yy)]
        return rc(at if src is None else src, at, yf_s.at[d, s], yf_r.at[d, s], yn[d])

    def ce(d, s, rows):
        at = lat_s.at[zc(d, s), rows, lanes(yl)]
        return rc(at, at, ce_s.at[d, s], ce_r.at[d, s], core)

    def co(d, s, rows):
        at = lat_s.at[zc(d, s), rows, lanes(1 - yl)]
        return rc(at, at, co_s.at[d, s], co_r.at[d, s], core)

    def wlanes(kk):
        return pl.ds(pl.multiple_of(kk * width, width), width)

    def zf(c, n, own=False):
        rows = pl.ds((n % pieces) * PIECE, PIECE)
        at = wab.at[c, rows, wlanes(k)]
        s = n // pieces
        return rc(w_ref.at[rows] if own else at, at, zf_s.at[s], zf_r.at[s], core)

    def zf_block(c, s, kk):
        at = wab.at[c, :, wlanes(kk)]
        return rc(at, at, zf_s.at[s], zf_r.at[s], core)

    def zw(d, n, back=0, own=False):
        rows = pl.ds((n % pieces) * PIECE, PIECE)
        at = wab.at[zc(d, n // pieces), rows, wlanes(k)]
        m = n - back
        return rc(w_ref.at[rows] if own else at, at, zw_s.at[d, m], zw_r.at[d, m], zn[d])

    def relay(n):
        s = n // pieces
        for d in range(2):
            @when(s >= 1, reaches(s, d))
            def _():
                zw(d, n, back=pieces).wait_recv()

                @pl.when(k != d if s < half else k == 0)
                def _():
                    zf(zc(d, s), n).start()

        @when(s == 0, k == 1)
        def _():
            zf(z, n, own=True).start()

        for d in range(2):
            @when(n >= FLIGHT, reaches((n - FLIGHT) // pieces + 1, d))
            def _():
                zw(d, n - FLIGHT).wait_send()

            @when(reaches(s + 1, d))
            def _():
                zw(d, n, own=s == 0).start()

    barrier = pltpu.get_barrier_semaphore()
    peers = [zn[0], zn[1], core, ypair_core] + [t for _, _, t in plane]
    for peer in peers:
        pl.semaphore_signal(barrier, inc=1, device_id=peer, device_id_type=MESH)
    pl.semaphore_wait(barrier, len(peers))

    for d in range(2):
        zl(d, 0, lat_ref.at[part_rows]).start()
    yf(0, 0, yl, lat_ref.at[half_rows]).start()
    relay(0)

    for side in range(2):
        @pl.when(yl == side)
        def _():
            lat_s[z, :, side * tok:(side + 1) * tok] = lat_ref[...]
    for side in range(2):
        @pl.when(k == side)
        def _():
            wab[z, :, side * width:(side + 1) * width] = w_ref[...]
    eye = (
        lax.broadcasted_iota(jnp.int32, (tok, tok), 0)
        == lax.broadcasted_iota(jnp.int32, (tok, tok), 1)
    ).astype(jnp.bfloat16)
    for h in range(heads):
        q_s[h * tok:(h + 1) * tok, :] = lax.dot_general(
            eye, q_ref[h], (((1,), (1,)), ((), ())), preferred_element_type=jnp.float32
        ).astype(jnp.bfloat16)
    m_s[...] = jnp.full_like(m_s, LOW)
    l_s[...] = jnp.zeros_like(l_s)
    acc[...] = jnp.zeros_like(acc)

    def attend(c, diagonal):
        scores = jnp.dot(
            q_s[...], lat_s[c], preferred_element_type=jnp.float32
        ) * (score_scale * LOG2E)
        if diagonal:
            row_pos = yl * tok + lax.broadcasted_iota(jnp.int32, scores.shape, 0) % tok
            key_pos = lax.broadcasted_iota(jnp.int32, scores.shape, 1)
            scores = jnp.where(key_pos <= row_pos, scores, LOW)
        old = m_s[...]
        new = jnp.maximum(old, jnp.max(scores, axis=1, keepdims=True))
        shrink = jnp.exp2(old - new)
        expo = jnp.exp2(scores - new)
        m_s[...] = new
        l_s[...] = l_s[...] * shrink + jnp.sum(expo, axis=1, keepdims=True)
        acc[...] = acc[...] * shrink + lax.dot_general(
            expo.astype(jnp.bfloat16), lat_s[c, :nvl], (((1,), (1,)), ((), ())),
            preferred_element_type=jnp.float32,
        )

    steps = half + 3

    begun = 1
    for s in range(1, steps + 1):
        for d in range(2):
            @when(reaches(s, d))
            def _():
                zl(d, s, back=1).wait_recv()

                @when(reaches(s + 1, d))
                def _():
                    zl(d, s).start()

                xl(d, s, part_rows).start()

        s1 = s - 1
        for d in range(2):
            @when(s1 >= 1, reaches(s1, d))
            def _():
                xl(d, s1, missing_rows).wait_recv()
                yf(d, s1, yl).start()
                ce(d, s1, half_rows).start()

        s2 = s - 2
        for d in range(2):
            @when(s2 >= 1 or (s2 == 0 and d == 0), s2 == 0 or reaches(s2, d))
            def _():
                yf(d, s2, 1 - yl).wait_recv()
                co(d, s2, half_rows).start()

        relay(begun)
        begun += 1

        s3 = s - 3
        for d in range(2):
            there = reaches(s3, 1 - d)

            @when(s3 >= 1, there)
            def _():
                ce(d, s3, other_rows).wait_recv()

            @when(s3 >= 1 or (s3 == 0 and d == 0), s3 == 0 or there)
            def _():
                co(d, s3, other_rows).wait_recv()

        if s3 == 0:
            attend(z, True)
        if s3 >= 1:
            @pl.loop(0, 2 if s3 < half else 1)
            def _(d):
                c = jnp.where(d == 0, z - s3, z + s3 - nz)

                @pl.when(c >= 0)
                def _():
                    attend(c, False)

        if s in EXTRA and begun < half * pieces:
            relay(begun)
            begun += 1

    made = []
    for h in range(heads):
        rows = pl.ds(h * tok, tok)
        context = (acc[rows, :] / l_s[rows, :]).astype(jnp.bfloat16)
        made.append(
            jnp.dot(context, up_ref[h], preferred_element_type=jnp.float32).astype(jnp.bfloat16)
        )
    made = jnp.concatenate(made, axis=1)
    for side in range(2):
        @pl.when(k == side)
        def _():
            vx[yl, :, side * width:(side + 1) * width] = made

    def v_copy(i, yy, kk):
        at = vx.at[yy, :, wlanes(kk)]
        return rc(at, at, v_s.at[i], v_r.at[i], (core, ypair, ypair_core)[i])

    for i in range(3):
        v_copy(i, yl, k).start()
    v_copy(0, yl, 1 - k).wait_recv()
    v_copy(1, 1 - yl, k).wait_recv()
    v_copy(2, 1 - yl, 1 - k).wait_recv()

    def steps_of(g, kk):
        return g + kk

    def block_of(g, kk):
        return jnp.where(kk == 0, zc(0, g), zc(1, g + 1))

    def f_copy(g):
        return rc(ts.at[g, 1 - k], fr.at[g], f_s.at[g], f_r.at[g], core)

    def r_all(g):
        return rc(xr.at[g], xr.at[g], r_s.at[g], r_r.at[g], core)

    def part(g):
        c = block_of(g, k)
        zf_block(c, steps_of(g, k), 1 - k).wait_recv()
        o = lax.dot_general(
            vx[...].reshape(2 * tok, 2 * width), wab[c], (((1,), (1,)), ((), ())),
            preferred_element_type=jnp.float32,
        ).astype(jnp.bfloat16)
        o = o.reshape(2, 2, nx, 16, ncol)
        for hi in range(2):
            for lo in range(2):
                ps[g, hi * 2 + lo] = o[lo, hi]
        for i in sorted(range(len(plane)), key=lambda i: -((i + 1) // nx == 2) - ((i + 1) % nx == 2)):
            yy, xx, to = plane[i]
            rc(ps.at[g, yy, xx], xr.at[g, i], r_s.at[g], r_r.at[g], to).start()

    def sum_plane(g):
        r_all(g).wait_recv()
        own, other = ps[g, y, x].astype(jnp.float32), None
        for i in range(4 * nx - 1):
            term = xr[g, i].astype(jnp.float32)
            if ((i + 1) // nx) % 2 == 0:
                own = own + term
            else:
                other = term if other is None else other + term
        for side, total in enumerate((own, other)):
            for kk in range(2):
                ts[g, kk, side] = total[kk * 8:(kk + 1) * 8].astype(ts.dtype)
        f_copy(g).start()
        c = block_of(g, k)
        out_ref[2 * c + yl] = ts[g, k, 0]
        out_ref[2 * c + 1 - yl] = ts[g, k, 1]

    def finish(g):
        f_copy(g).wait_recv()
        c = block_of(g, 1 - k)
        out_ref[2 * c + yl] = fr[g, 0]
        out_ref[2 * c + 1 - yl] = fr[g, 1]

    relays = list(range(begun, half * pieces + pieces))
    ready_after = [max(0, (g + 2) * pieces - begun) for g in range(half)]
    stages = {"part": part, "sum": sum_plane, "end": finish, "relay": relay}
    for name, index in order_of(relays, half, ready_after):
        stages[name](index)

    for s in range(half + 1):
        for d in range(2):
            @when(reaches(s + 1, d))
            def _():
                zl(d, s).wait_send()

            @when(s >= 1, reaches(s, d))
            def _():
                xl(d, s, part_rows).wait_send()
                ce(d, s, half_rows).wait_send()

            @when(s >= 1 or d == 0, s == 0 or reaches(s, d))
            def _():
                yf(d, s, yl).wait_send()
                co(d, s, half_rows).wait_send()

    for i in range(3):
        v_copy(i, yl, k).wait_send()

    for g in range(half):
        zf_block(block_of(g, 1 - k), steps_of(g, 1 - k), k).wait_send()
        r_all(g).wait_send()
        f_copy(g).wait_send()


def shards(queries, latents, value_up, out_weight):
    nz = lax.axis_size("ctx") // 2
    nx = lax.axis_size("exp") // 4
    tok, heads, lat = queries.shape
    nvl, vd = value_up.shape[1], value_up.shape[2]
    rows = tok * heads
    width = heads * vd
    ncol = out_weight.shape[1]
    half = nz // 2
    ng = half
    bf, f32 = jnp.bfloat16, jnp.float32
    dma = pltpu.SemaphoreType.DMA
    vmem = pl.BlockSpec(memory_space=pltpu.VMEM)
    out = pl.pallas_call(
        functools.partial(kernel, nz, nx, nvl),
        out_shape=jax.ShapeDtypeStruct((2 * nz, 8, ncol), bf),
        in_specs=[vmem] * 4,
        out_specs=vmem,
        scratch_shapes=[
            pltpu.VMEM((rows, lat), bf),
            pltpu.VMEM((nz, lat, 2 * tok), bf),
            pltpu.VMEM((nz, ncol, 2 * width), bf),
            pltpu.VMEM((rows, 1), f32),
            pltpu.VMEM((rows, 1), f32),
            pltpu.VMEM((rows, nvl), f32),
            pltpu.VMEM((2, tok, 2 * width), bf),
            pltpu.VMEM((ng, 4, nx, 16, ncol), bf),
            pltpu.VMEM((ng, 4 * nx - 1, 16, ncol), bf),
            pltpu.VMEM((ng, 2, 2, 8, ncol), bf),
            pltpu.VMEM((ng, 2, 8, ncol), bf),
        ]
        + [dma((2, half + 1))] * 10
        + [dma((2, half * (ncol // PIECE)))] * 2
        + [dma((half + 1,))] * 2
        + [dma((3,))] * 2
        + [dma((ng,))] * 4,
        compiler_params=pltpu.CompilerParams(
            collective_id=0, has_side_effects=True, vmem_limit_bytes=56 * 2**20
        ),
        name="latent_attention",
    )(jnp.transpose(queries, (1, 2, 0)), latents.T, value_up, out_weight.T)
    return jnp.moveaxis(out, 1, 0).reshape(8, 2 * nz * ncol)


def solution(mesh):
    in_specs = (P("ctx", "exp", None), P("ctx", None), P("exp", None, None), P("exp", "ctx"))
    out_specs = P(("ctx", "exp"), None)
    return jax.shard_map(shards, mesh=mesh, in_specs=in_specs, out_specs=out_specs, check_vma=False)
```
